32 devices in a mesh: block: 8 (over y, x, core), tok: 4 (over z).
Axes of the slice: x: 2, y: 2, z: 4, core: 2. Of those that a mesh axis runs over, the one named last changes fastest.
Arguments:
- queries: bfloat16 [8192, 1536], P(('block', 'tok')), may hold values from -6 to 6
- key_rows: bfloat16 [8192, 1536], P(('block', 'tok')), may hold values from -6 to 6
- value_rows: bfloat16 [8192, 1536], P(('block', 'tok')), may hold values from -6 to 6
- step_rates: float32 [8192, 4], P(('block', 'tok')), may hold values from 0.000637888 to 0.005103104
- fast_in: float32 [8, 4, 3, 384, 384], P('block', None, None, 'tok'), may hold values from -2 to 2
Outputs:
- applied: bfloat16 [8192, 1536], P(('block', 'tok'))
- handed: float32 [8, 4, 3, 384, 384], P('block', None, None, 'tok')
The draws below stay inside these ranges and needn't reach their ends.
All inputs are finite; a program needn't handle non-finite values.
Results may differ from the reference program's by a relative error of at most 0.03.
Values may be sent and summed in bfloat16 or wider, within the bound.
No kernel may reach another device: no remote copies, remote signals or barrier semaphores. Data moves between devices by JAX's collectives and lax.ppermute only.
A program may use at most 64 MiB of HBM per device.

```python
import math
import jax
import jax.numpy as jnp
from jax import lax

H = 4
HD = 384
TOK_DEV = 256
NCH = 8
CTOK = 1024
TOKENS = 8192
N_TOK = 4


def draw_fast_in(key, part):
    first, second = jax.random.split(jax.random.fold_in(key, 7), 2)
    shape_all = (NCH, H, 3, HD, HD)
    position = jnp.arange(HD, dtype=jnp.float32) / (HD - 1) - 0.5
    base = jnp.clip(jax.random.normal(first, shape_all, jnp.float32), -4.0, 4.0)
    ramp = jnp.exp(jnp.log(3.0) * position)
    rough = jnp.exp(jax.random.uniform(second, (NCH, H, 3, HD, 1), jnp.float32, -0.35, 0.35))
    weights = base * ramp[:, None] * rough / jnp.sqrt(jnp.float32(HD))
    return jnp.clip(weights, -2.0, 2.0).astype(jnp.float32)


def block_levels(stream_key, extent, shards, smallest, high):
    factor_of = 1.0
    for dim, blocks in shards:
        heights = jax.random.uniform(jax.random.fold_in(jax.random.fold_in(stream_key, 6), dim), (blocks,), jnp.float32, smallest / len(shards), high / len(shards))
        factor_of = factor_of * jnp.repeat(jnp.exp(heights), extent[dim] // blocks).reshape((-1,) + (1,) * (len(extent) - 1 - dim))
    return factor_of


def gaussian(stream_key, dims, scale, most, cuts=(), held_as=jnp.bfloat16):
    gain = block_levels(stream_key, dims, cuts, -0.22, 0.18) if cuts else 1.0
    entries = jax.random.normal(stream_key, dims, jnp.float32) * scale * gain
    return jnp.minimum(jnp.maximum(entries, -most), most).astype(held_as)


def setup_inputs(seed: int = 0) -> dict:
    key_of = jax.random.split(jax.random.key(seed), 6)
    queries = gaussian(key_of[0], (TOKENS, H * HD), 1.0, 6.0, ((0, 32),))
    key_rows = gaussian(key_of[1], (TOKENS, H * HD), 1.0, 6.0, ((0, 32),))
    value_rows = gaussian(key_of[2], (TOKENS, H * HD), 1.0, 6.0, ((0, 32),))
    step_rates = jnp.clip(jnp.exp(math.log(0.005103104) - 2.0794415 * jax.random.uniform(key_of[3], (TOKENS, H), jnp.float32) ** block_levels(key_of[3], (TOKENS, H), ((0, 32),), -0.2, 0.2)), 0.000637888, 0.005103104)
    fast_in = draw_fast_in(jax.random.fold_in(key_of[5], 71), 0)
    return dict(queries=queries, key_rows=key_rows, value_rows=value_rows, step_rates=step_rates, fast_in=fast_in)


epsilon = 1e-06

def rounded(value):
    return lax.optimization_barrier(value.astype(jnp.bfloat16)).astype(jnp.float32)

def fast_grads(key_heads, value_heads, rate_heads, weights):
    gate_pre = jnp.einsum('thi,hij->thj', key_heads, weights[:, 0])
    up_pre = jnp.einsum('thi,hij->thj', key_heads, weights[:, 1])
    sig_gate = jax.nn.sigmoid(gate_pre)
    activated = gate_pre * sig_gate
    hidden = rounded(activated * up_pre)
    target = rounded(-(rate_heads[:, :, None] * value_heads))
    back_hidden = jnp.einsum('tho,hjo->thj', target, weights[:, 2])
    grad_gate = rounded(back_hidden * up_pre * sig_gate * (1.0 + gate_pre * (1.0 - sig_gate)))
    grad_up = rounded(back_hidden * activated)
    first = jnp.einsum('thi,thj->hij', key_heads, grad_gate)
    third = jnp.einsum('thi,thj->hij', key_heads, grad_up)
    second = jnp.einsum('thj,tho->hjo', hidden, target)
    return rounded(jnp.stack([first, third, second], axis=1))

def block_step(inputs):
    query_part, key_part, value_part, rate_part, start_weights = inputs
    weights = rounded(start_weights)
    group_grads = jax.vmap(lambda kk, vv, ee: fast_grads(kk, vv, ee, weights))(key_part, value_part, rate_part)
    grad_sum = lax.optimization_barrier(jnp.sum(group_grads, axis=0))
    stepped = start_weights - grad_sum
    old_sq = lax.optimization_barrier(jnp.sum(start_weights * start_weights, axis=2))
    new_sq = lax.optimization_barrier(jnp.sum(stepped * stepped, axis=2))
    renewed = stepped * jnp.sqrt((old_sq + epsilon) / (new_sq + epsilon))[:, :, None, :]
    fresh_b = rounded(renewed)
    query_flat = query_part.reshape(CTOK, H, HD)
    gate_pre = jnp.einsum('thi,hij->thj', query_flat, fresh_b[:, 0])
    up_pre = jnp.einsum('thi,hij->thj', query_flat, fresh_b[:, 1])
    hidden = rounded(jax.nn.silu(gate_pre) * up_pre)
    result = jnp.einsum('thj,hjo->tho', hidden, fresh_b[:, 2])
    return (result.reshape(CTOK, H * HD).astype(jnp.bfloat16), renewed)

def reference(queries, key_rows, value_rows, step_rates, fast_in):
    shape_rows = (NCH, N_TOK, TOK_DEV, H, HD)
    query_all = queries.astype(jnp.float32).reshape(shape_rows)
    key_all = key_rows.astype(jnp.float32).reshape(shape_rows)
    value_all = value_rows.astype(jnp.float32).reshape(shape_rows)
    rate_all = step_rates.astype(jnp.float32).reshape(NCH, N_TOK, TOK_DEV, H)
    applied, renewed = lax.map(block_step, (query_all, key_all, value_all, rate_all, fast_in))
    applied = applied.reshape(TOKENS, H * HD)
    handed = jnp.roll(renewed, 1, axis=0)
    return (applied, handed)
```

```python
import functools

import jax
import jax.numpy as jnp
from jax import lax
from jax.experimental import pallas as pl
from jax.experimental.pallas import tpu as pltpu
from jax.sharding import PartitionSpec as P

epsilon = 1e-06


def shifted(block, axis, distance):
    devices = range(lax.axis_size(axis))
    route = [((i - distance) % len(devices), i) for i in devices]
    return lax.ppermute(block, axis, route)


def fast_grads(key_rows, value_rows, step_rates, weights):
    token_count = key_rows.shape[0]
    head_count = weights.shape[0]
    head_width = weights.shape[-1]
    key_heads = key_rows.reshape(token_count, head_count, head_width)
    value_heads = value_rows.reshape(token_count, head_count, head_width)
    gate_pre = jnp.einsum(
        "thi,hij->thj", key_heads, weights[:, 0], preferred_element_type=jnp.float32
    )
    up_pre = jnp.einsum(
        "thi,hij->thj", key_heads, weights[:, 1], preferred_element_type=jnp.float32
    )
    sig_gate = jax.nn.sigmoid(gate_pre)
    activated = gate_pre * sig_gate
    hidden = (activated * up_pre).astype(jnp.bfloat16)
    target = (-(step_rates[:, :, None] * value_heads.astype(jnp.float32))).astype(jnp.bfloat16)
    back_hidden = jnp.einsum(
        "tho,hjo->thj", target, weights[:, 2], preferred_element_type=jnp.float32
    )
    grad_gate = (back_hidden * up_pre * sig_gate * (1.0 + gate_pre * (1.0 - sig_gate))).astype(
        jnp.bfloat16
    )
    grad_up = (back_hidden * activated).astype(jnp.bfloat16)
    first = jnp.einsum("thi,thj->hij", key_heads, grad_gate, preferred_element_type=jnp.float32)
    third = jnp.einsum("thi,thj->hij", key_heads, grad_up, preferred_element_type=jnp.float32)
    second = jnp.einsum("thj,tho->hjo", hidden, target, preferred_element_type=jnp.float32)
    return jnp.stack([first, third, second], axis=1)


def apply_heads(queries, weights):
    token_count = queries.shape[0]
    head_count = weights.shape[0]
    head_width = weights.shape[-1]
    query_heads = queries.reshape(token_count, head_count, head_width)
    gate_pre = jnp.einsum(
        "thi,hij->thj", query_heads, weights[:, 0], preferred_element_type=jnp.float32
    )
    up_pre = jnp.einsum(
        "thi,hij->thj", query_heads, weights[:, 1], preferred_element_type=jnp.float32
    )
    hidden = (jax.nn.silu(gate_pre) * up_pre).astype(jnp.bfloat16)
    result = jnp.einsum("thj,hjo->tho", hidden, weights[:, 2], preferred_element_type=jnp.float32)
    return result.reshape(token_count, head_count * head_width).astype(jnp.bfloat16)


def gathered_body(queries, key_rows, value_rows, step_rates, fast_in):
    own_weights = fast_in[0]
    shard_rows = own_weights.shape[2]
    whole_weights = lax.all_gather(
        own_weights.astype(jnp.bfloat16), "tok", axis=2, tiled=True
    ).astype(own_weights.dtype)
    grads = fast_grads(key_rows, value_rows, step_rates, whole_weights.astype(jnp.bfloat16))
    grad_sum = lax.psum(grads.astype(jnp.bfloat16), "tok").astype(jnp.float32)
    stepped = whole_weights - grad_sum
    old_sq = jnp.sum(whole_weights * whole_weights, axis=2)
    new_sq = jnp.sum(stepped * stepped, axis=2)
    renewed_full = stepped * jnp.sqrt((old_sq + epsilon) / (new_sq + epsilon))[:, :, None, :]
    applied = apply_heads(queries, renewed_full.astype(jnp.bfloat16))
    renewed = lax.dynamic_slice_in_dim(
        renewed_full, lax.axis_index("tok") * shard_rows, shard_rows, 2
    )
    handed = shifted(renewed[None].astype(jnp.bfloat16), "block", 1).astype(jnp.float32)
    return (applied, handed)


def call(kernel, outs, scratch, scalar, args, flops=0):
    moved = sum(a.size * a.dtype.itemsize for a in (*args, *outs))
    spec = pl.BlockSpec(memory_space=pltpu.VMEM)
    return pl.pallas_call(
        kernel,
        out_shape=outs,
        in_specs=[pl.BlockSpec(memory_space=pltpu.SMEM)] + [spec] * len(args),
        out_specs=[spec] * len(outs),
        scratch_shapes=scratch,
        compiler_params=pltpu.CompilerParams(vmem_limit_bytes=48 << 20),
        cost_estimate=pl.CostEstimate(flops=flops, bytes_accessed=moved, transcendentals=0),
    )(scalar, *args)


def head_of(place_ref, step, heads):
    return lax.rem(place_ref[0] + step, heads)


def pack_kernel(heads, place_ref, key_ref, value_ref, rate_ref, weight_ref, query_ref, *out_refs):
    width = weight_ref.shape[-1]
    tokens = key_ref.shape[0]
    rates = rate_ref[...]
    column = lax.broadcasted_iota(jnp.int32, rates.shape, 1)
    for step in range(heads):
        head = head_of(place_ref, step, heads)
        at = pl.ds(pl.multiple_of(head * width, 128), width)
        message, query_out = out_refs[step], out_refs[heads + step]
        message[:tokens] = key_ref[:, at]
        rate = jnp.sum(jnp.where(column == head, rates, 0.0), axis=1, keepdims=True)
        value = value_ref[:, at].astype(jnp.float32)
        message[tokens : 2 * tokens] = (-(rate * value)).astype(jnp.bfloat16)
        matrices, rows = weight_ref.shape[1], weight_ref.shape[2]
        for m in range(matrices):
            start = 2 * tokens + m * rows
            message[start : start + rows] = weight_ref[head, m].astype(jnp.bfloat16)
        query_out[...] = query_ref[:, at]


def transposed_dot(a, b):
    return lax.dot_general(a, b, (((0,), (0,)), ((), ())), preferred_element_type=jnp.float32)


def renew_kernel(heads, tokens, rows, place_ref, *refs):
    message_refs = refs[:heads]
    full_ref, handed_refs = refs[heads], refs[heads + 1 : 2 * heads + 1]
    weights, keys, targets, gates, hiddens = refs[2 * heads + 1 :]
    width = full_ref.shape[-1]
    for step in range(heads):
        source = lax.rem(place_ref[0] + heads - step, heads)
        at = pl.ds(pl.multiple_of(source * rows, 16), rows)
        for m in range(3):
            start = 2 * tokens + m * rows
            weights[m, at] = message_refs[step][start : start + rows]
        keys[step * tokens : (step + 1) * tokens] = message_refs[step][:tokens]
        targets[step * tokens : (step + 1) * tokens] = message_refs[step][tokens : 2 * tokens]
    for step in range(heads):
        at = slice(step * tokens, (step + 1) * tokens)
        key, target = keys[at], targets[at]
        gate_pre = jnp.dot(key, weights[0], preferred_element_type=jnp.float32)
        up_pre = jnp.dot(key, weights[1], preferred_element_type=jnp.float32)
        back = lax.dot_general(
            target, weights[2], (((1,), (1,)), ((), ())), preferred_element_type=jnp.float32
        )
        sig_gate = jax.nn.sigmoid(gate_pre)
        activated = gate_pre * sig_gate
        hiddens[at] = (activated * up_pre).astype(jnp.bfloat16)
        gates[at, :width] = (back * up_pre * sig_gate * (1.0 + gate_pre * (1.0 - sig_gate))).astype(
            jnp.bfloat16
        )
        gates[at, width:] = (back * activated).astype(jnp.bfloat16)
    key_grads = transposed_dot(keys[...], gates[...])
    grads = (
        key_grads[:, :width],
        key_grads[:, width:],
        transposed_dot(hiddens[...], targets[...]),
    )
    for m in range(3):
        old = weights[m].astype(jnp.float32)
        stepped = old - grads[m]
        old_sq = jnp.sum(old * old, axis=0, keepdims=True)
        new_sq = jnp.sum(stepped * stepped, axis=0, keepdims=True)
        full_ref[m] = (stepped * jnp.sqrt((old_sq + epsilon) / (new_sq + epsilon))).astype(
            jnp.bfloat16
        )
    for step in range(heads):
        at = pl.ds(pl.multiple_of(head_of(place_ref, step, heads) * rows, 16), rows)
        for m in range(3):
            handed_refs[step][m] = full_ref[m, at]


def apply_kernel(heads, place_ref, full_ref, *refs):
    for query_ref, out_ref in zip(refs[:heads], refs[heads:]):
        query = query_ref[...]
        gate_pre = jnp.dot(query, full_ref[0], preferred_element_type=jnp.float32)
        up_pre = jnp.dot(query, full_ref[1], preferred_element_type=jnp.float32)
        hidden = (gate_pre * jax.nn.sigmoid(gate_pre) * up_pre).astype(jnp.bfloat16)
        out_ref[...] = jnp.dot(hidden, full_ref[2], preferred_element_type=jnp.float32).astype(
            jnp.bfloat16
        )


def handed_kernel(heads, place_ref, *refs):
    handed_ref = refs[heads]
    for step in range(heads):
        head = lax.rem(place_ref[0] + heads - step, heads)
        handed_ref[0, head] = refs[step][...].astype(jnp.float32)


def applied_kernel(heads, place_ref, *refs):
    applied_ref = refs[heads]
    width = refs[0].shape[-1]
    for step in range(heads):
        head = head_of(place_ref, step, heads)
        applied_ref[:, pl.ds(pl.multiple_of(head * width, 128), width)] = refs[step][...]


def head_body(queries, key_rows, value_rows, step_rates, fast_in):
    _, heads, matrices, rows, width = fast_in.shape
    tokens = queries.shape[0]
    blocks = lax.axis_size("block")
    place = lax.axis_index("tok").astype(jnp.int32)[None]
    bf16 = functools.partial(jax.ShapeDtypeStruct, dtype=jnp.bfloat16)
    step_flops = 2 * heads * tokens * width * width

    packed = call(
        functools.partial(pack_kernel, heads),
        [bf16((2 * tokens + matrices * rows, width))] * heads + [bf16((tokens, width))] * heads,
        [],
        place,
        (key_rows, value_rows, step_rates, fast_in[0], queries),
    )
    messages = [packed[0]] + [shifted(packed[d], "tok", d) for d in range(1, heads)]
    messages, query_out = lax.optimization_barrier((messages, packed[heads:]))
    query_in = [query_out[0]] + [shifted(query_out[d], "tok", d) for d in range(1, heads)]

    full, *handed_out = call(
        functools.partial(renew_kernel, heads, tokens, rows),
        [bf16((matrices, width, width))] + [bf16((matrices, rows, width))] * heads,
        [
            pltpu.VMEM((matrices, width, width), jnp.bfloat16),
            pltpu.VMEM((heads * tokens, width), jnp.bfloat16),
            pltpu.VMEM((heads * tokens, width), jnp.bfloat16),
            pltpu.VMEM((heads * tokens, 2 * width), jnp.bfloat16),
            pltpu.VMEM((heads * tokens, width), jnp.bfloat16),
        ],
        place,
        messages,
        6 * step_flops,
    )
    handed_in = []
    for d in range(heads):
        route = [
            (b * heads + z, ((b + 1) % blocks) * heads + (z + d) % heads)
            for b in range(blocks)
            for z in range(heads)
        ]
        handed_in.append(lax.ppermute(handed_out[d], ("block", "tok"), route))
    result_out = call(
        functools.partial(apply_kernel, heads),
        [bf16((tokens, width))] * heads,
        [],
        place,
        (full, *query_in),
        3 * step_flops,
    )
    result_in = [result_out[0]] + [shifted(result_out[d], "tok", -d) for d in range(1, heads)]
    (handed,) = call(
        functools.partial(handed_kernel, heads),
        [jax.ShapeDtypeStruct((1, heads, matrices, rows, width), jnp.float32)],
        [],
        place,
        handed_in,
    )
    (applied,) = call(
        functools.partial(applied_kernel, heads),
        [bf16((tokens, heads * width))],
        [],
        place,
        result_in,
    )
    return (applied, handed)


def body(queries, key_rows, value_rows, step_rates, fast_in):
    by_head = fast_in.shape[1] == lax.axis_size("tok")
    chosen = head_body if by_head else gathered_body
    return chosen(queries, key_rows, value_rows, step_rates, fast_in)


def solution(mesh):
    return jax.shard_map(
        body,
        mesh=mesh,
        in_specs=(
            P(("block", "tok"), None),
            P(("block", "tok"), None),
            P(("block", "tok"), None),
            P(("block", "tok"), None),
            P("block", None, None, "tok", None),
        ),
        out_specs=(P(("block", "tok"), None), P("block", None, None, "tok", None)),
        check_vma=False,
    )
```

```python
import functools

import jax
import jax.numpy as jnp
from jax import lax
from jax.experimental import pallas as pl
from jax.experimental.pallas import tpu as pltpu
from jax.sharding import PartitionSpec as P


epsilon = 1e-06


def shifted(block, axis, distance):
    devices = range(lax.axis_size(axis))
    route = [((i - distance) % len(devices), i) for i in devices]
    return lax.ppermute(block, axis, route)


def fast_grads(key_rows, value_rows, step_rates, weights):
    token_count = key_rows.shape[0]
    head_count = weights.shape[0]
    head_width = weights.shape[-1]
    key_heads = key_rows.reshape(token_count, head_count, head_width)
    value_heads = value_rows.reshape(token_count, head_count, head_width)
    gate_pre = jnp.einsum(
        "thi,hij->thj", key_heads, weights[:, 0], preferred_element_type=jnp.float32
    )
    up_pre = jnp.einsum(
        "thi,hij->thj", key_heads, weights[:, 1], preferred_element_type=jnp.float32
    )
    sig_gate = jax.nn.sigmoid(gate_pre)
    activated = gate_pre * sig_gate
    hidden = (activated * up_pre).astype(jnp.bfloat16)
    target = (-(step_rates[:, :, None] * value_heads.astype(jnp.float32))).astype(jnp.bfloat16)
    back_hidden = jnp.einsum(
        "tho,hjo->thj", target, weights[:, 2], preferred_element_type=jnp.float32
    )
    grad_gate = (back_hidden * up_pre * sig_gate * (1.0 + gate_pre * (1.0 - sig_gate))).astype(
        jnp.bfloat16
    )
    grad_up = (back_hidden * activated).astype(jnp.bfloat16)
    first = jnp.einsum("thi,thj->hij", key_heads, grad_gate, preferred_element_type=jnp.float32)
    third = jnp.einsum("thi,thj->hij", key_heads, grad_up, preferred_element_type=jnp.float32)
    second = jnp.einsum("thj,tho->hjo", hidden, target, preferred_element_type=jnp.float32)
    return jnp.stack([first, third, second], axis=1)


def apply_heads(queries, weights):
    token_count = queries.shape[0]
    head_count = weights.shape[0]
    head_width = weights.shape[-1]
    query_heads = queries.reshape(token_count, head_count, head_width)
    gate_pre = jnp.einsum(
        "thi,hij->thj", query_heads, weights[:, 0], preferred_element_type=jnp.float32
    )
    up_pre = jnp.einsum(
        "thi,hij->thj", query_heads, weights[:, 1], preferred_element_type=jnp.float32
    )
    hidden = (jax.nn.silu(gate_pre) * up_pre).astype(jnp.bfloat16)
    result = jnp.einsum("thj,hjo->tho", hidden, weights[:, 2], preferred_element_type=jnp.float32)
    return result.reshape(token_count, head_count * head_width).astype(jnp.bfloat16)


def gathered_body(queries, key_rows, value_rows, step_rates, fast_in):
    own_weights = fast_in[0]
    shard_rows = own_weights.shape[2]
    whole_weights = lax.all_gather(
        own_weights.astype(jnp.bfloat16), "tok", axis=2, tiled=True
    ).astype(own_weights.dtype)
    grads = fast_grads(key_rows, value_rows, step_rates, whole_weights.astype(jnp.bfloat16))
    grad_sum = lax.psum(grads.astype(jnp.bfloat16), "tok").astype(jnp.float32)
    stepped = whole_weights - grad_sum
    old_sq = jnp.sum(whole_weights * whole_weights, axis=2)
    new_sq = jnp.sum(stepped * stepped, axis=2)
    renewed_full = stepped * jnp.sqrt((old_sq + epsilon) / (new_sq + epsilon))[:, :, None, :]
    applied = apply_heads(queries, renewed_full.astype(jnp.bfloat16))
    renewed = lax.dynamic_slice_in_dim(
        renewed_full, lax.axis_index("tok") * shard_rows, shard_rows, 2
    )
    handed = shifted(renewed[None].astype(jnp.bfloat16), "block", 1).astype(jnp.float32)
    return (applied, handed)


def call(kernel, outs, scratch, place, args, flops=0, kept=(), limit=40):
    moved = sum(a.size * a.dtype.itemsize for a in (*args, *outs))
    spec = pl.BlockSpec(memory_space=pltpu.VMEM)
    far = pl.BlockSpec(memory_space=pltpu.HBM)
    return pl.pallas_call(
        kernel,
        out_shape=outs,
        in_specs=[pl.BlockSpec(memory_space=pltpu.SMEM)]
        + [far if i in kept else spec for i in range(len(args))],
        out_specs=[spec] * len(outs),
        scratch_shapes=scratch,
        compiler_params=pltpu.CompilerParams(vmem_limit_bytes=limit << 20),
        cost_estimate=pl.CostEstimate(flops=flops, bytes_accessed=moved, transcendentals=0),
    )(place, *args)


def rows_dot(a, b):
    return lax.dot_general(a, b, (((0,), (0,)), ((), ())), preferred_element_type=jnp.float32)


def columns_dot(a, b):
    return lax.dot_general(a, b, (((1,), (1,)), ((), ())), preferred_element_type=jnp.float32)


def plain_dot(a, b):
    return jnp.dot(a, b, preferred_element_type=jnp.float32)


LANES = 128


def span(start, size, unit):
    return pl.ds(pl.multiple_of(start, unit), size)


class Sizes:
    def __init__(self, tokens, rows, width):
        self.tokens, self.rows, self.width = tokens, rows, width
        self.blocks = width // LANES
        self.target_at = self.blocks * tokens
        self.down_at = 2 * self.blocks * tokens
        self.gate_at = self.down_at + self.blocks * rows
        self.first_end = self.gate_at + 2 * rows
        self.late = 2 * (self.blocks - 1) * rows
        self.query_at = self.first_end + self.late
        self.mate_end = self.query_at + 2 * self.blocks * tokens
        self.late_width = width - LANES


def pack_kernel(sizes, place_ref, *refs):
    far, outs, near, sems = refs[:5], refs[5:12], refs[12:17], refs[17]
    own_ref, mate_ref, cross_ref, cross_late_ref, other_ref, other_late_ref, query_ref = outs
    copies = [pltpu.make_async_copy(far[i], near[i], sems.at[i]) for i in range(5)]
    for copy in copies:
        copy.start()
    rate_ref, key_ref, value_ref, weight_ref, queries_ref = near
    tokens, rows, width, blocks = sizes.tokens, sizes.rows, sizes.width, sizes.blocks
    here = place_ref[0]
    parts = (
        (here ^ 1, mate_ref, (mate_ref, sizes.first_end)),
        (here ^ 3, cross_ref, (cross_late_ref, 0)),
        (here ^ 2, other_ref, (other_late_ref, 0)),
        (here, own_ref, (own_ref, sizes.first_end)),
    )
    copies[0].wait()
    copies[1].wait()
    for head, message, _ in parts:
        for c in range(blocks):
            at = span(head * width + c * LANES, LANES, LANES)
            message[c * tokens : (c + 1) * tokens] = key_ref[:, at]
    rates = rate_ref[...]
    row = lax.broadcasted_iota(jnp.int32, rates.shape, 0)
    copies[2].wait()
    for head, message, _ in parts:
        rate = jnp.sum(jnp.where(row == head, rates, 0.0), axis=0, keepdims=True)
        rate = jnp.broadcast_to(rate, (LANES, tokens)).T
        for c in range(blocks):
            at = span(head * width + c * LANES, LANES, LANES)
            start = sizes.target_at + c * tokens
            value = value_ref[:, at].astype(jnp.float32)
            message[start : start + tokens] = (-(rate * value)).astype(jnp.bfloat16)
    copies[3].wait()
    for head, message, (late, late_at) in parts:
        for m in range(2):
            start = sizes.gate_at + m * rows
            message[start : start + rows] = weight_ref[head, m, :, :LANES].astype(jnp.bfloat16)
            for c in range(1, blocks):
                start = late_at + (m * (blocks - 1) + c - 1) * rows
                late[start : start + rows] = weight_ref[
                    head, m, :, c * LANES : (c + 1) * LANES
                ].astype(jnp.bfloat16)
        for c in range(blocks):
            start = sizes.down_at + c * rows
            message[start : start + rows] = weight_ref[
                head, 2, :, c * LANES : (c + 1) * LANES
            ].astype(jnp.bfloat16)
    copies[4].wait()
    for i, head in enumerate((here ^ 1, here ^ 3)):
        for c in range(blocks):
            at = span(head * width + c * LANES, LANES, LANES)
            start = sizes.query_at + (i * blocks + c) * tokens
            mate_ref[start : start + tokens] = queries_ref[:, at]
    for i, head in enumerate((here, here ^ 2)):
        query_ref[i] = queries_ref[:, span(head * width, width, LANES)]


def pre_grads(pre, back, half):
    gate_pre, up_pre = pre[:, :half], pre[:, half:]
    sig_gate = jax.nn.sigmoid(gate_pre)
    activated = gate_pre * sig_gate
    hidden = (activated * up_pre).astype(jnp.bfloat16)
    gate = (back * up_pre * sig_gate * (1.0 + gate_pre * (1.0 - sig_gate))).astype(jnp.bfloat16)
    return hidden, gate, (back * activated).astype(jnp.bfloat16)


def renewal(old, grad):
    old = old.astype(jnp.float32)
    stepped = old - grad
    old_sq = jnp.sum(old * old, axis=0, keepdims=True)
    new_sq = jnp.sum(stepped * stepped, axis=0, keepdims=True)
    return (stepped * jnp.sqrt((old_sq + epsilon) / (new_sq + epsilon))).astype(jnp.bfloat16)


def quarters(here):
    return (here, here ^ 1, here ^ 3, here ^ 2)


def first_kernel(sizes, place_ref, *refs):
    messages = refs[:4]
    keys, targets, down, hidden_ref, first_ref, weights, gates = refs[4:]
    tokens, rows, blocks = sizes.tokens, sizes.rows, sizes.blocks
    for g, (source, message) in enumerate(zip(quarters(place_ref[0]), messages)):
        at = span(source * rows, rows, 16)
        mine = slice(g * tokens, (g + 1) * tokens)
        for m in range(2):
            start = sizes.gate_at + m * rows
            weights[at, m * LANES : (m + 1) * LANES] = message[start : start + rows]
        for c in range(blocks):
            lanes = slice(c * LANES, (c + 1) * LANES)
            keys[mine, lanes] = message[c * tokens : (c + 1) * tokens]
            start = sizes.target_at + c * tokens
            targets[mine, lanes] = message[start : start + tokens]
            start = sizes.down_at + c * rows
            down[at, lanes] = message[start : start + rows]
    for g in range(4):
        mine = slice(g * tokens, (g + 1) * tokens)
        pre = plain_dot(keys[mine], weights[...])
        back = columns_dot(targets[mine], down[:LANES])
        hidden_ref[mine], gates[mine, :LANES], gates[mine, LANES:] = pre_grads(pre, back, LANES)
    first_ref[...] = renewal(weights[...], rows_dot(keys[...], gates[...]))


def second_kernel(sizes, place_ref, *refs):
    keys, targets, down, early, first, own, mate, cross, other = refs[:9]
    late_ref, down_ref, near_ref, far0_ref, far1_ref, same_ref, mate_ref = refs[9:16]
    weights, gates, hidden = refs[16:]
    tokens, rows, blocks, late = sizes.tokens, sizes.rows, sizes.blocks, sizes.late_width
    here = place_ref[0]
    starts = (sizes.first_end, sizes.first_end, 0, 0)
    for source, message, start in zip(quarters(here), (own, mate, cross, other), starts):
        at = span(source * rows, rows, 16)
        for i in range(2 * (blocks - 1)):
            weights[at, i * LANES : (i + 1) * LANES] = message[
                start + i * rows : start + (i + 1) * rows
            ]
    hidden[:, :LANES] = early[...]
    for g in range(4):
        mine = slice(g * tokens, (g + 1) * tokens)
        pre = plain_dot(keys[mine], weights[...])
        back = columns_dot(targets[mine], down[LANES:])
        hidden[mine, LANES:], gates[mine, :late], gates[mine, late:] = pre_grads(pre, back, late)
    late_ref[...] = renewal(weights[...], rows_dot(keys[...], gates[...]))
    down_ref[...] = renewal(down[...], rows_dot(hidden[...], targets[...]))
    half = lax.shift_right_logical(here, 1)
    near_ref[...] = down_ref[span((1 - half) * 2 * rows, 2 * rows, 16)]
    far = span(half * 2 * rows, 2 * rows, 16)
    far0_ref[...] = down_ref[far, :late]
    far1_ref[...] = down_ref[far, late:]
    for ref, row in ((same_ref, here), (mate_ref, here ^ 1)):
        at = span(row * rows, rows, 16)
        hand_rows(ref, at, first, late_ref, late)
        ref[2] = down_ref[at]


def hand_rows(ref, at, first, second, late):
    for m in range(2):
        ref[m, :, :LANES] = first[at, m * LANES : (m + 1) * LANES]
        ref[m, :, LANES:] = second[at, m * late : (m + 1) * late]


def hidden_of(query, first, second, late):
    pre, pre_late = plain_dot(query, first[...]), plain_dot(query, second[...])
    gate, up = pre[:, :LANES], pre[:, LANES:]
    gate_late, up_late = pre_late[:, :late], pre_late[:, late:]
    return (
        (gate * jax.nn.sigmoid(gate) * up).astype(jnp.bfloat16),
        (gate_late * jax.nn.sigmoid(gate_late) * up_late).astype(jnp.bfloat16),
    )


def mate_query(sizes, mate, i):
    tokens, blocks = sizes.tokens, sizes.blocks
    start = sizes.query_at + i * blocks * tokens
    return jnp.concatenate(
        [mate[start + c * tokens : start + (c + 1) * tokens] for c in range(blocks)], axis=1
    )


def own_kernel(sizes, place_ref, query, mate, first, second, down, own_ref, mate_ref):
    late = sizes.late_width
    for tokens, ref in ((mate_query(sizes, mate, 0), mate_ref), (query[0], own_ref)):
        early, after = hidden_of(tokens, first, second, late)
        result = plain_dot(early, down[:LANES]) + plain_dot(after, down[LANES:])
        ref[...] = result.astype(jnp.bfloat16)


def other_kernel(sizes, place_ref, *refs):
    query, mate, first, second, near = refs[:5]
    hidden_ref, same_ref, mate_ref = refs[5:]
    late, rows, tokens = sizes.late_width, sizes.rows, sizes.tokens
    here = place_ref[0]
    for ref, row in ((mate_ref, here ^ 1), (same_ref, here)):
        hand_rows(ref, span(row * rows, rows, 16), first, second, late)
        ref[2] = near[span((row & 1) * rows, rows, 16)]
    for g, q in enumerate((mate_query(sizes, mate, 1), query[1])):
        mine = slice(g * tokens, (g + 1) * tokens)
        hidden_ref[mine, :LANES], hidden_ref[mine, LANES:] = hidden_of(q, first, second, late)


def result_kernel(sizes, start, place_ref, hidden, near, far, own_ref, mate_ref, down):
    half = lax.shift_right_logical(place_ref[0], 1)
    rows, tokens, columns = 2 * sizes.rows, sizes.tokens, far.shape[-1]
    down[span(half * rows, rows, 16)] = near[:, start : start + columns]
    down[span((1 - half) * rows, rows, 16)] = far[...]
    mate_ref[...] = plain_dot(hidden[:tokens], down[...]).astype(jnp.bfloat16)
    own_ref[...] = plain_dot(hidden[tokens:], down[...]).astype(jnp.bfloat16)


def handed_kernel(place_ref, *refs):
    here = place_ref[0]
    for head, ref in zip((here, here ^ 1, here ^ 2, here ^ 3), refs[:4]):
        refs[4][0, head] = ref[...].astype(jnp.float32)


def applied_kernel(sizes, place_ref, own, mate, own0, own1, mate0, mate1, applied_ref):
    here, width, late = place_ref[0], sizes.width, sizes.late_width
    applied_ref[:, span(here * width, width, LANES)] = own[...]
    applied_ref[:, span((here ^ 1) * width, width, LANES)] = mate[...]
    for head, (first, second) in ((here ^ 2, (own0, own1)), (here ^ 3, (mate0, mate1))):
        applied_ref[:, span(head * width, late, LANES)] = first[...]
        applied_ref[:, span(head * width + late, LANES, LANES)] = second[...]


def head_body(queries, key_rows, value_rows, step_rates, fast_in):
    _, heads, matrices, rows, width = fast_in.shape
    tokens = queries.shape[0]
    blocks = lax.axis_size("block")
    place = lax.axis_index("tok").astype(jnp.int32)[None]
    sizes = Sizes(tokens, rows, width)
    late = sizes.late_width
    flops = 2 * tokens * width * width

    def bf16(*shape):
        return jax.ShapeDtypeStruct(shape, jnp.bfloat16)

    def swapped(value, mask):
        return lax.ppermute(value, "tok", [(i, i ^ mask) for i in range(heads)])

    def next_block(value, mask):
        route = [
            (b * heads + z, ((b + 1) % blocks) * heads + (z ^ mask))
            for b in range(blocks)
            for z in range(heads)
        ]
        return lax.ppermute(value, ("block", "tok"), route)

    arrays = (step_rates.T, key_rows, value_rows, fast_in[0], queries)
    own, mate, cross, cross_late, other, other_late, query = call(
        functools.partial(pack_kernel, sizes),
        [
            bf16(sizes.query_at, LANES),
            bf16(sizes.mate_end, LANES),
            bf16(sizes.first_end, LANES),
            bf16(sizes.late, LANES),
            bf16(sizes.first_end, LANES),
            bf16(sizes.late, LANES),
            bf16(2, tokens, width),
        ],
        [pltpu.VMEM(a.shape, a.dtype) for a in arrays] + [pltpu.SemaphoreType.DMA((5,))],
        place,
        arrays,
        kept=range(5),
        limit=40,
    )
    mate = swapped(mate, 1)
    cross = swapped(cross, 3)
    other = swapped(other, 2)
    cross_late = swapped(cross_late, 3)
    other_late = swapped(other_late, 2)

    keys, targets, down, early, first = call(
        functools.partial(first_kernel, sizes),
        [
            bf16(heads * tokens, width),
            bf16(heads * tokens, width),
            bf16(width, width),
            bf16(heads * tokens, LANES),
            bf16(width, 2 * LANES),
        ],
        [
            pltpu.VMEM((width, 2 * LANES), jnp.bfloat16),
            pltpu.VMEM((heads * tokens, 2 * LANES), jnp.bfloat16),
        ],
        place,
        (own, mate, cross, other),
        6 * heads * flops // 3,
    )
    first_in = swapped(first, 2)
    second, down, near, far0, far1, same_rows, mate_rows = call(
        functools.partial(second_kernel, sizes),
        [
            bf16(width, 2 * late),
            bf16(width, width),
            bf16(2 * rows, width),
            bf16(2 * rows, late),
            bf16(2 * rows, LANES),
            bf16(matrices, rows, width),
            bf16(matrices, rows, width),
        ],
        [
            pltpu.VMEM((width, 2 * late), jnp.bfloat16),
            pltpu.VMEM((heads * tokens, 2 * late), jnp.bfloat16),
            pltpu.VMEM((heads * tokens, width), jnp.bfloat16),
        ],
        place,
        (keys, targets, down, early, first, own, mate, cross_late, other_late),
        12 * heads * flops // 3,
    )
    second_in = swapped(second, 2)
    near_in = swapped(near, 2)
    far0_in = swapped(far0, 2)
    far1_in = swapped(far1, 2)
    own_result, mate_result = call(
        functools.partial(own_kernel, sizes),
        [bf16(tokens, width)] * 2,
        [],
        place,
        (query, mate, first, second, down),
        6 * flops,
    )
    mate_result = swapped(mate_result, 1)
    handed_own = next_block(same_rows, 0)
    handed_mate = next_block(mate_rows, 1)

    hidden, same_rows, mate_rows = call(
        functools.partial(other_kernel, sizes),
        [bf16(2 * tokens, width), bf16(matrices, rows, width), bf16(matrices, rows, width)],
        [],
        place,
        (query, mate, first_in, second_in, near_in),
        4 * flops,
    )
    handed_cross = next_block(mate_rows, 1)
    handed_other = next_block(same_rows, 0)
    own_parts, mate_parts = [], []
    for i, far in enumerate((far0_in, far1_in)):
        columns = far.shape[-1]
        own_part, mate_part = call(
            functools.partial(result_kernel, sizes, i * late),
            [bf16(tokens, columns)] * 2,
            [pltpu.VMEM((width, columns), jnp.bfloat16)],
            place,
            (hidden, near_in, far),
            2 * flops * columns // width,
        )
        own_parts.append(own_part)
        mate_parts.append(swapped(mate_part, 1))
    (handed,) = call(
        handed_kernel,
        [jax.ShapeDtypeStruct((1, heads, matrices, rows, width), jnp.float32)],
        [],
        place,
        (handed_own, handed_mate, handed_other, handed_cross),
    )
    (applied,) = call(
        functools.partial(applied_kernel, sizes),
        [bf16(tokens, heads * width)],
        [],
        place,
        (own_result, mate_result, *own_parts, *mate_parts),
    )
    return (applied, handed)


def body(queries, key_rows, value_rows, step_rates, fast_in):
    by_head = fast_in.shape[1] == lax.axis_size("tok") == 4
    chosen = head_body if by_head else gathered_body
    return chosen(queries, key_rows, value_rows, step_rates, fast_in)


def solution(mesh):
    return jax.shard_map(
        body,
        mesh=mesh,
        in_specs=(
            P(("block", "tok"), None),
            P(("block", "tok"), None),
            P(("block", "tok"), None),
            P(("block", "tok"), None),
            P("block", None, None, "tok", None),
        ),
        out_specs=(P(("block", "tok"), None), P("block", None, None, "tok", None)),
        check_vma=False,
    )
```

```python
import functools

import jax
import jax.numpy as jnp
from jax import lax
from jax.experimental import pallas as pl
from jax.experimental.pallas import tpu as pltpu
from jax.sharding import PartitionSpec as P


epsilon = 1e-06


def shifted(block, axis, distance):
    devices = range(lax.axis_size(axis))
    route = [((i - distance) % len(devices), i) for i in devices]
    return lax.ppermute(block, axis, route)


def fast_grads(key_rows, value_rows, step_rates, weights):
    token_count = key_rows.shape[0]
    head_count = weights.shape[0]
    head_width = weights.shape[-1]
    key_heads = key_rows.reshape(token_count, head_count, head_width)
    value_heads = value_rows.reshape(token_count, head_count, head_width)
    gate_pre = jnp.einsum(
        "thi,hij->thj", key_heads, weights[:, 0], preferred_element_type=jnp.float32
    )
    up_pre = jnp.einsum(
        "thi,hij->thj", key_heads, weights[:, 1], preferred_element_type=jnp.float32
    )
    sig_gate = jax.nn.sigmoid(gate_pre)
    activated = gate_pre * sig_gate
    hidden = (activated * up_pre).astype(jnp.bfloat16)
    target = (-(step_rates[:, :, None] * value_heads.astype(jnp.float32))).astype(jnp.bfloat16)
    back_hidden = jnp.einsum(
        "tho,hjo->thj", target, weights[:, 2], preferred_element_type=jnp.float32
    )
    grad_gate = (back_hidden * up_pre * sig_gate * (1.0 + gate_pre * (1.0 - sig_gate))).astype(
        jnp.bfloat16
    )
    grad_up = (back_hidden * activated).astype(jnp.bfloat16)
    first = jnp.einsum("thi,thj->hij", key_heads, grad_gate, preferred_element_type=jnp.float32)
    third = jnp.einsum("thi,thj->hij", key_heads, grad_up, preferred_element_type=jnp.float32)
    second = jnp.einsum("thj,tho->hjo", hidden, target, preferred_element_type=jnp.float32)
    return jnp.stack([first, third, second], axis=1)


def apply_heads(queries, weights):
    token_count = queries.shape[0]
    head_count = weights.shape[0]
    head_width = weights.shape[-1]
    query_heads = queries.reshape(token_count, head_count, head_width)
    gate_pre = jnp.einsum(
        "thi,hij->thj", query_heads, weights[:, 0], preferred_element_type=jnp.float32
    )
    up_pre = jnp.einsum(
        "thi,hij->thj", query_heads, weights[:, 1], preferred_element_type=jnp.float32
    )
    hidden = (jax.nn.silu(gate_pre) * up_pre).astype(jnp.bfloat16)
    result = jnp.einsum("thj,hjo->tho", hidden, weights[:, 2], preferred_element_type=jnp.float32)
    return result.reshape(token_count, head_count * head_width).astype(jnp.bfloat16)


def gathered_body(queries, key_rows, value_rows, step_rates, fast_in):
    own_weights = fast_in[0]
    shard_rows = own_weights.shape[2]
    whole_weights = lax.all_gather(
        own_weights.astype(jnp.bfloat16), "tok", axis=2, tiled=True
    ).astype(own_weights.dtype)
    grads = fast_grads(key_rows, value_rows, step_rates, whole_weights.astype(jnp.bfloat16))
    grad_sum = lax.psum(grads.astype(jnp.bfloat16), "tok").astype(jnp.float32)
    stepped = whole_weights - grad_sum
    old_sq = jnp.sum(whole_weights * whole_weights, axis=2)
    new_sq = jnp.sum(stepped * stepped, axis=2)
    renewed_full = stepped * jnp.sqrt((old_sq + epsilon) / (new_sq + epsilon))[:, :, None, :]
    applied = apply_heads(queries, renewed_full.astype(jnp.bfloat16))
    renewed = lax.dynamic_slice_in_dim(
        renewed_full, lax.axis_index("tok") * shard_rows, shard_rows, 2
    )
    handed = shifted(renewed[None].astype(jnp.bfloat16), "block", 1).astype(jnp.float32)
    return (applied, handed)


def call(kernel, outs, scratch, place, args, flops=0, kept=(), limit=40):
    moved = sum(a.size * a.dtype.itemsize for a in (*args, *outs))
    spec = pl.BlockSpec(memory_space=pltpu.VMEM)
    far = pl.BlockSpec(memory_space=pltpu.HBM)
    run = pl.pallas_call(
        kernel,
        out_shape=outs,
        in_specs=[pl.BlockSpec(memory_space=pltpu.SMEM)]
        + [far if i in kept else spec for i in range(len(args))],
        out_specs=[spec] * len(outs),
        scratch_shapes=scratch,
        compiler_params=pltpu.CompilerParams(vmem_limit_bytes=limit << 20),
        cost_estimate=pl.CostEstimate(flops=flops, bytes_accessed=moved, transcendentals=0),
    )
    args = [
        pltpu.with_memory_space_constraint(a, pltpu.HBM) if i in kept else a
        for i, a in enumerate(args)
    ]
    return run(place, *args)


def rows_dot(a, b):
    return lax.dot_general(a, b, (((0,), (0,)), ((), ())), preferred_element_type=jnp.float32)


def columns_dot(a, b):
    return lax.dot_general(a, b, (((1,), (1,)), ((), ())), preferred_element_type=jnp.float32)


def plain_dot(a, b):
    return jnp.dot(a, b, preferred_element_type=jnp.float32)


LANES = 128


def span(start, size, unit):
    return pl.ds(pl.multiple_of(start, unit), size)


class Sizes:
    def __init__(self, tokens, rows, width):
        self.tokens, self.rows, self.width = tokens, rows, width
        self.blocks = width // LANES
        self.target_at = self.blocks * tokens
        self.down_at = 2 * self.blocks * tokens
        self.gate_at = self.down_at + self.blocks * rows
        self.first_end = self.gate_at + 2 * rows
        self.late = 2 * (self.blocks - 1) * rows
        self.query_at = self.first_end + self.late
        self.mate_end = self.query_at + 2 * self.blocks * tokens
        self.late_width = width - LANES


def pack_kernel(sizes, place_ref, *refs):
    far, outs, near, sems = refs[:5], refs[5:12], refs[12:17], refs[17]
    own_ref, mate_ref, cross_ref, cross_late_ref, other_ref, other_late_ref, query_ref = outs
    copies = [pltpu.make_async_copy(far[i], near[i], sems.at[i]) for i in range(5)]
    for copy in copies:
        copy.start()
    rate_ref, key_ref, value_ref, weight_ref, queries_ref = near
    tokens, rows, width, blocks = sizes.tokens, sizes.rows, sizes.width, sizes.blocks
    here = place_ref[0]
    parts = (
        (here ^ 1, mate_ref, (mate_ref, sizes.first_end)),
        (here ^ 3, cross_ref, (cross_late_ref, 0)),
        (here ^ 2, other_ref, (other_late_ref, 0)),
        (here, own_ref, (own_ref, sizes.first_end)),
    )
    copies[0].wait()
    copies[1].wait()
    for head, message, _ in parts:
        for c in range(blocks):
            at = span(head * width + c * LANES, LANES, LANES)
            message[c * tokens : (c + 1) * tokens] = key_ref[:, at]
    rates = rate_ref[...]
    row = lax.broadcasted_iota(jnp.int32, rates.shape, 0)
    copies[2].wait()
    for head, message, _ in parts:
        rate = jnp.sum(jnp.where(row == head, rates, 0.0), axis=0, keepdims=True)
        rate = jnp.broadcast_to(rate, (LANES, tokens)).T
        for c in range(blocks):
            at = span(head * width + c * LANES, LANES, LANES)
            start = sizes.target_at + c * tokens
            value = value_ref[:, at].astype(jnp.float32)
            message[start : start + tokens] = (-(rate * value)).astype(jnp.bfloat16)
    copies[3].wait()
    for head, message, (late, late_at) in parts:
        for m in range(2):
            start = sizes.gate_at + m * rows
            message[start : start + rows] = weight_ref[head, m, :, :LANES].astype(jnp.bfloat16)
            for c in range(1, blocks):
                start = late_at + (m * (blocks - 1) + c - 1) * rows
                late[start : start + rows] = weight_ref[
                    head, m, :, c * LANES : (c + 1) * LANES
                ].astype(jnp.bfloat16)
        for c in range(blocks):
            start = sizes.down_at + c * rows
            message[start : start + rows] = weight_ref[
                head, 2, :, c * LANES : (c + 1) * LANES
            ].astype(jnp.bfloat16)
    copies[4].wait()
    for i, head in enumerate((here ^ 1, here ^ 3)):
        for c in range(blocks):
            at = span(head * width + c * LANES, LANES, LANES)
            start = sizes.query_at + (i * blocks + c) * tokens
            mate_ref[start : start + tokens] = queries_ref[:, at]
    for i, head in enumerate((here, here ^ 2)):
        query_ref[i] = queries_ref[:, span(head * width, width, LANES)]


def pre_grads(pre, back, half):
    gate_pre, up_pre = pre[:, :half], pre[:, half:]
    sig_gate = jax.nn.sigmoid(gate_pre)
    activated = gate_pre * sig_gate
    hidden = (activated * up_pre).astype(jnp.bfloat16)
    gate = (back * up_pre * sig_gate * (1.0 + gate_pre * (1.0 - sig_gate))).astype(jnp.bfloat16)
    return hidden, gate, (back * activated).astype(jnp.bfloat16)


def renewal(old, grad):
    old = old.astype(jnp.float32)
    stepped = old - grad
    old_sq = jnp.sum(old * old, axis=0, keepdims=True)
    new_sq = jnp.sum(stepped * stepped, axis=0, keepdims=True)
    return (stepped * jnp.sqrt((old_sq + epsilon) / (new_sq + epsilon))).astype(jnp.bfloat16)


def quarters(here):
    return (here, here ^ 1, here ^ 3, here ^ 2)


def first_kernel(sizes, place_ref, *refs):
    messages = refs[:4]
    keys, targets, down, hidden_ref, first_ref, weights, gates = refs[4:]
    tokens, rows, blocks = sizes.tokens, sizes.rows, sizes.blocks
    for g, (source, message) in enumerate(zip(quarters(place_ref[0]), messages)):
        at = span(source * rows, rows, 16)
        mine = slice(g * tokens, (g + 1) * tokens)
        for m in range(2):
            start = sizes.gate_at + m * rows
            weights[at, m * LANES : (m + 1) * LANES] = message[start : start + rows]
        for c in range(blocks):
            lanes = slice(c * LANES, (c + 1) * LANES)
            keys[mine, lanes] = message[c * tokens : (c + 1) * tokens]
            start = sizes.target_at + c * tokens
            targets[mine, lanes] = message[start : start + tokens]
            start = sizes.down_at + c * rows
            down[at, lanes] = message[start : start + rows]
    for g in range(4):
        mine = slice(g * tokens, (g + 1) * tokens)
        pre = plain_dot(keys[mine], weights[...])
        back = columns_dot(targets[mine], down[:LANES])
        hidden_ref[mine], gates[mine, :LANES], gates[mine, LANES:] = pre_grads(pre, back, LANES)
    first_ref[...] = renewal(weights[...], rows_dot(keys[...], gates[...]))


def second_kernel(sizes, place_ref, *refs):
    keys, targets, down, early, first, own, mate, cross, other = refs[:9]
    late_ref, down_ref, near_ref, far_ref, far0_ref, far1_ref, same_ref, mate_ref = refs[9:17]
    weights, gates, hidden = refs[17:]
    tokens, rows, blocks, late = sizes.tokens, sizes.rows, sizes.blocks, sizes.late_width
    here = place_ref[0]
    starts = (sizes.first_end, sizes.first_end, 0, 0)
    for source, message, start in zip(quarters(here), (own, mate, cross, other), starts):
        at = span(source * rows, rows, 16)
        for i in range(2 * (blocks - 1)):
            weights[at, i * LANES : (i + 1) * LANES] = message[
                start + i * rows : start + (i + 1) * rows
            ]
    hidden[:, :LANES] = early[...]
    for g in range(4):
        mine = slice(g * tokens, (g + 1) * tokens)
        pre = plain_dot(keys[mine], weights[...])
        back = columns_dot(targets[mine], down[LANES:])
        hidden[mine, LANES:], gates[mine, :late], gates[mine, late:] = pre_grads(pre, back, late)
    late_ref[...] = renewal(weights[...], rows_dot(keys[...], gates[...]))
    down_ref[...] = renewal(down[...], rows_dot(hidden[...], targets[...]))
    half = lax.shift_right_logical(here, 1)
    near = span((1 - half) * 2 * rows, 2 * rows, 16)
    far = span(half * 2 * rows, 2 * rows, 16)
    near_ref[:, : 2 * late] = late_ref[near]
    near_ref[:, 2 * late :] = down_ref[near]
    far_ref[...] = late_ref[far]
    far0_ref[...] = down_ref[far, :late]
    far1_ref[...] = down_ref[far, late:]
    for ref, row in ((same_ref, here), (mate_ref, here ^ 1)):
        at = span(row * rows, rows, 16)
        hand_rows(ref, at, first, late_ref, late)
        ref[2] = down_ref[at]


def hand_rows(ref, at, first, second, late):
    for m in range(2):
        ref[m, :, :LANES] = first[at, m * LANES : (m + 1) * LANES]
        ref[m, :, LANES:] = second[at, m * late : (m + 1) * late]


def hidden_of(query, first, second, late):
    pre, pre_late = plain_dot(query, first[...]), plain_dot(query, second[...])
    gate, up = pre[:, :LANES], pre[:, LANES:]
    gate_late, up_late = pre_late[:, :late], pre_late[:, late:]
    return (
        (gate * jax.nn.sigmoid(gate) * up).astype(jnp.bfloat16),
        (gate_late * jax.nn.sigmoid(gate_late) * up_late).astype(jnp.bfloat16),
    )


def mate_query(sizes, mate, i):
    tokens, blocks = sizes.tokens, sizes.blocks
    start = sizes.query_at + i * blocks * tokens
    return jnp.concatenate(
        [mate[start + c * tokens : start + (c + 1) * tokens] for c in range(blocks)], axis=1
    )


def own_kernel(sizes, place_ref, query, mate, first, second, down, own_ref, mate_ref):
    late = sizes.late_width
    for tokens, ref in ((mate_query(sizes, mate, 0), mate_ref), (query[0], own_ref)):
        early, after = hidden_of(tokens, first, second, late)
        result = plain_dot(early, down[:LANES]) + plain_dot(after, down[LANES:])
        ref[...] = result.astype(jnp.bfloat16)


def rows_kernel(sizes, place_ref, first, near, same_ref, mate_ref):
    late, rows, here = sizes.late_width, sizes.rows, place_ref[0]
    for ref, row in ((mate_ref, here ^ 1), (same_ref, here)):
        at = span(row * rows, rows, 16)
        arrived = span((row & 1) * rows, rows, 16)
        for m in range(2):
            ref[m, :, :LANES] = first[at, m * LANES : (m + 1) * LANES]
            ref[m, :, LANES:] = near[arrived, m * late : (m + 1) * late]
        ref[2] = near[arrived, 2 * late :]


def halves(sizes, here):
    half, rows = lax.shift_right_logical(here, 1), 2 * sizes.rows
    return span(half * rows, rows, 16), span((1 - half) * rows, rows, 16)


def other_kernel(sizes, place_ref, query, mate, first, near, far, hidden_ref, second):
    late, tokens = sizes.late_width, sizes.tokens
    near_at, far_at = halves(sizes, place_ref[0])
    second[near_at] = near[:, : 2 * late]
    second[far_at] = far[...]
    for g, q in enumerate((mate_query(sizes, mate, 1), query[1])):
        mine = slice(g * tokens, (g + 1) * tokens)
        hidden_ref[mine, :LANES], hidden_ref[mine, LANES:] = hidden_of(q, first, second, late)


def result_kernel(sizes, start, place_ref, hidden, near, far, own_ref, mate_ref, down):
    tokens, columns = sizes.tokens, far.shape[-1]
    start += 2 * sizes.late_width
    near_at, far_at = halves(sizes, place_ref[0])
    down[near_at] = near[:, start : start + columns]
    down[far_at] = far[...]
    mate_ref[...] = plain_dot(hidden[:tokens], down[...]).astype(jnp.bfloat16)
    own_ref[...] = plain_dot(hidden[tokens:], down[...]).astype(jnp.bfloat16)


def handed_kernel(place_ref, *refs):
    here = place_ref[0]
    for head, ref in zip((here, here ^ 1, here ^ 2, here ^ 3), refs[:4]):
        refs[4][0, head] = ref[...].astype(jnp.float32)


def applied_kernel(sizes, place_ref, own, mate, own0, own1, mate0, mate1, applied_ref):
    here, width, late = place_ref[0], sizes.width, sizes.late_width
    applied_ref[:, span(here * width, width, LANES)] = own[...]
    applied_ref[:, span((here ^ 1) * width, width, LANES)] = mate[...]
    for head, (first, second) in ((here ^ 2, (own0, own1)), (here ^ 3, (mate0, mate1))):
        applied_ref[:, span(head * width, late, LANES)] = first[...]
        applied_ref[:, span(head * width + late, LANES, LANES)] = second[...]


def head_body(queries, key_rows, value_rows, step_rates, fast_in):
    _, heads, matrices, rows, width = fast_in.shape
    tokens = queries.shape[0]
    blocks = lax.axis_size("block")
    place = lax.axis_index("tok").astype(jnp.int32)[None]
    sizes = Sizes(tokens, rows, width)
    late = sizes.late_width
    flops = 2 * tokens * width * width

    def bf16(*shape):
        return jax.ShapeDtypeStruct(shape, jnp.bfloat16)

    def swapped(value, mask):
        return lax.ppermute(value, "tok", [(i, i ^ mask) for i in range(heads)])

    def next_block(value, mask):
        route = [
            (b * heads + z, ((b + 1) % blocks) * heads + (z ^ mask))
            for b in range(blocks)
            for z in range(heads)
        ]
        return lax.ppermute(value, ("block", "tok"), route)

    arrays = (step_rates.T, key_rows, value_rows, fast_in[0], queries)
    own, mate, cross, cross_late, other, other_late, query = call(
        functools.partial(pack_kernel, sizes),
        [
            bf16(sizes.query_at, LANES),
            bf16(sizes.mate_end, LANES),
            bf16(sizes.first_end, LANES),
            bf16(sizes.late, LANES),
            bf16(sizes.first_end, LANES),
            bf16(sizes.late, LANES),
            bf16(2, tokens, width),
        ],
        [pltpu.VMEM(a.shape, a.dtype) for a in arrays] + [pltpu.SemaphoreType.DMA((5,))],
        place,
        arrays,
        kept=range(5),
        limit=40,
    )
    mate = swapped(mate, 1)
    cross = swapped(cross, 3)
    other = swapped(other, 2)
    cross_late = swapped(cross_late, 3)
    other_late = swapped(other_late, 2)

    keys, targets, down, early, first = call(
        functools.partial(first_kernel, sizes),
        [
            bf16(heads * tokens, width),
            bf16(heads * tokens, width),
            bf16(width, width),
            bf16(heads * tokens, LANES),
            bf16(width, 2 * LANES),
        ],
        [
            pltpu.VMEM((width, 2 * LANES), jnp.bfloat16),
            pltpu.VMEM((heads * tokens, 2 * LANES), jnp.bfloat16),
        ],
        place,
        (own, mate, cross, other),
        6 * heads * flops // 3,
    )
    first_in = swapped(first, 2)
    second, down, near, far, far0, far1, same_rows, mate_rows = call(
        functools.partial(second_kernel, sizes),
        [
            bf16(width, 2 * late),
            bf16(width, width),
            bf16(2 * rows, 2 * late + width),
            bf16(2 * rows, 2 * late),
            bf16(2 * rows, late),
            bf16(2 * rows, LANES),
            bf16(matrices, rows, width),
            bf16(matrices, rows, width),
        ],
        [
            pltpu.VMEM((width, 2 * late), jnp.bfloat16),
            pltpu.VMEM((heads * tokens, 2 * late), jnp.bfloat16),
            pltpu.VMEM((heads * tokens, width), jnp.bfloat16),
        ],
        place,
        (keys, targets, down, early, first, own, mate, cross_late, other_late),
        12 * heads * flops // 3,
    )
    near_in = swapped(near, 2)
    far_in = swapped(far, 2)
    far0_in = swapped(far0, 2)
    far1_in = swapped(far1, 2)
    own_result, mate_result = call(
        functools.partial(own_kernel, sizes),
        [bf16(tokens, width)] * 2,
        [],
        place,
        (query, mate, first, second, down),
        6 * flops,
    )
    mate_result = swapped(mate_result, 1)
    handed_own = next_block(same_rows, 0)
    handed_mate = next_block(mate_rows, 1)

    same_rows, mate_rows = call(
        functools.partial(rows_kernel, sizes),
        [bf16(matrices, rows, width)] * 2,
        [],
        place,
        (first_in, near_in),
    )
    handed_cross = next_block(mate_rows, 1)
    handed_other = next_block(same_rows, 0)
    (hidden,) = call(
        functools.partial(other_kernel, sizes),
        [bf16(2 * tokens, width)],
        [pltpu.VMEM((width, 2 * late), jnp.bfloat16)],
        place,
        (query, mate, first_in, near_in, far_in),
        4 * flops,
    )
    own_parts, mate_parts = [], []
    for i, far in enumerate((far0_in, far1_in)):
        columns = far.shape[-1]
        own_part, mate_part = call(
            functools.partial(result_kernel, sizes, i * late),
            [bf16(tokens, columns)] * 2,
            [pltpu.VMEM((width, columns), jnp.bfloat16)],
            place,
            (hidden, near_in, far),
            2 * flops * columns // width,
        )
        own_parts.append(own_part)
        mate_parts.append(swapped(mate_part, 1))
    (handed,) = call(
        handed_kernel,
        [jax.ShapeDtypeStruct((1, heads, matrices, rows, width), jnp.float32)],
        [],
        place,
        (handed_own, handed_mate, handed_other, handed_cross),
    )
    (applied,) = call(
        functools.partial(applied_kernel, sizes),
        [bf16(tokens, heads * width)],
        [],
        place,
        (own_result, mate_result, *own_parts, *mate_parts),
    )
    return (applied, handed)


def body(queries, key_rows, value_rows, step_rates, fast_in):
    by_head = fast_in.shape[1] == lax.axis_size("tok") == 4
    chosen = head_body if by_head else gathered_body
    return chosen(queries, key_rows, value_rows, step_rates, fast_in)


def solution(mesh):
    return jax.shard_map(
        body,
        mesh=mesh,
        in_specs=(
            P(("block", "tok"), None),
            P(("block", "tok"), None),
            P(("block", "tok"), None),
            P(("block", "tok"), None),
            P("block", None, None, "tok", None),
        ),
        out_specs=(P(("block", "tok"), None), P("block", None, None, "tok", None)),
        check_vma=False,
    )
```

```python
import functools

import jax
import jax.numpy as jnp
from jax import lax
from jax.experimental import pallas as pl
from jax.experimental.pallas import tpu as pltpu
from jax.sharding import PartitionSpec as P


epsilon = 1e-06


def shifted(block, axis, distance):
    devices = range(lax.axis_size(axis))
    route = [((i - distance) % len(devices), i) for i in devices]
    return lax.ppermute(block, axis, route)


def fast_grads(key_rows, value_rows, step_rates, weights):
    token_count = key_rows.shape[0]
    head_count = weights.shape[0]
    head_width = weights.shape[-1]
    key_heads = key_rows.reshape(token_count, head_count, head_width)
    value_heads = value_rows.reshape(token_count, head_count, head_width)
    gate_pre = jnp.einsum(
        "thi,hij->thj", key_heads, weights[:, 0], preferred_element_type=jnp.float32
    )
    up_pre = jnp.einsum(
        "thi,hij->thj", key_heads, weights[:, 1], preferred_element_type=jnp.float32
    )
    sig_gate = jax.nn.sigmoid(gate_pre)
    activated = gate_pre * sig_gate
    hidden = (activated * up_pre).astype(jnp.bfloat16)
    target = (-(step_rates[:, :, None] * value_heads.astype(jnp.float32))).astype(jnp.bfloat16)
    back_hidden = jnp.einsum(
        "tho,hjo->thj", target, weights[:, 2], preferred_element_type=jnp.float32
    )
    grad_gate = (back_hidden * up_pre * sig_gate * (1.0 + gate_pre * (1.0 - sig_gate))).astype(
        jnp.bfloat16
    )
    grad_up = (back_hidden * activated).astype(jnp.bfloat16)
    first = jnp.einsum("thi,thj->hij", key_heads, grad_gate, preferred_element_type=jnp.float32)
    third = jnp.einsum("thi,thj->hij", key_heads, grad_up, preferred_element_type=jnp.float32)
    second = jnp.einsum("thj,tho->hjo", hidden, target, preferred_element_type=jnp.float32)
    return jnp.stack([first, third, second], axis=1)


def apply_heads(queries, weights):
    token_count = queries.shape[0]
    head_count = weights.shape[0]
    head_width = weights.shape[-1]
    query_heads = queries.reshape(token_count, head_count, head_width)
    gate_pre = jnp.einsum(
        "thi,hij->thj", query_heads, weights[:, 0], preferred_element_type=jnp.float32
    )
    up_pre = jnp.einsum(
        "thi,hij->thj", query_heads, weights[:, 1], preferred_element_type=jnp.float32
    )
    hidden = (jax.nn.silu(gate_pre) * up_pre).astype(jnp.bfloat16)
    result = jnp.einsum("thj,hjo->tho", hidden, weights[:, 2], preferred_element_type=jnp.float32)
    return result.reshape(token_count, head_count * head_width).astype(jnp.bfloat16)


def gathered_body(queries, key_rows, value_rows, step_rates, fast_in):
    own_weights = fast_in[0]
    shard_rows = own_weights.shape[2]
    whole_weights = lax.all_gather(
        own_weights.astype(jnp.bfloat16), "tok", axis=2, tiled=True
    ).astype(own_weights.dtype)
    grads = fast_grads(key_rows, value_rows, step_rates, whole_weights.astype(jnp.bfloat16))
    grad_sum = lax.psum(grads.astype(jnp.bfloat16), "tok").astype(jnp.float32)
    stepped = whole_weights - grad_sum
    old_sq = jnp.sum(whole_weights * whole_weights, axis=2)
    new_sq = jnp.sum(stepped * stepped, axis=2)
    renewed_full = stepped * jnp.sqrt((old_sq + epsilon) / (new_sq + epsilon))[:, :, None, :]
    applied = apply_heads(queries, renewed_full.astype(jnp.bfloat16))
    renewed = lax.dynamic_slice_in_dim(
        renewed_full, lax.axis_index("tok") * shard_rows, shard_rows, 2
    )
    handed = shifted(renewed[None].astype(jnp.bfloat16), "block", 1).astype(jnp.float32)
    return (applied, handed)


def call(kernel, outs, scratch, place, args, flops=0, kept=(), limit=40):
    moved = sum(a.size * a.dtype.itemsize for a in (*args, *outs))
    spec = pl.BlockSpec(memory_space=pltpu.VMEM)
    far = pl.BlockSpec(memory_space=pltpu.HBM)
    run = pl.pallas_call(
        kernel,
        out_shape=outs,
        in_specs=[pl.BlockSpec(memory_space=pltpu.SMEM)]
        + [far if i in kept else spec for i in range(len(args))],
        out_specs=[spec] * len(outs),
        scratch_shapes=scratch,
        compiler_params=pltpu.CompilerParams(vmem_limit_bytes=limit << 20),
        cost_estimate=pl.CostEstimate(flops=flops, bytes_accessed=moved, transcendentals=0),
    )
    args = [
        pltpu.with_memory_space_constraint(a, pltpu.HBM) if i in kept else a
        for i, a in enumerate(args)
    ]
    return run(place, *args)


def rows_dot(a, b):
    return lax.dot_general(a, b, (((0,), (0,)), ((), ())), preferred_element_type=jnp.float32)


def columns_dot(a, b):
    return lax.dot_general(a, b, (((1,), (1,)), ((), ())), preferred_element_type=jnp.float32)


def plain_dot(a, b):
    return jnp.dot(a, b, preferred_element_type=jnp.float32)


LANES = 128


def span(start, size, unit):
    return pl.ds(pl.multiple_of(start, unit), size)


class Sizes:
    def __init__(self, tokens, rows, width):
        self.tokens, self.rows, self.width = tokens, rows, width
        self.blocks = width // LANES
        self.target_at = self.blocks * tokens
        self.down_at = 2 * self.blocks * tokens
        self.gate_at = self.down_at + self.blocks * rows
        self.first_end = self.gate_at + 2 * rows
        self.late = 2 * (self.blocks - 1) * rows
        self.query_at = self.first_end + self.late
        self.mate_end = self.query_at + 2 * self.blocks * tokens
        self.late_width = width - LANES


def pack_kernel(sizes, place_ref, *refs):
    far, outs, near, sems = refs[:5], refs[5:12], refs[12:17], refs[17]
    own_ref, mate_ref, cross_ref, cross_late_ref, other_ref, other_late_ref, query_ref = outs
    copies = [pltpu.make_async_copy(far[i], near[i], sems.at[i]) for i in range(5)]
    for copy in copies:
        copy.start()
    rate_ref, key_ref, value_ref, weight_ref, queries_ref = near
    tokens, rows, width, blocks = sizes.tokens, sizes.rows, sizes.width, sizes.blocks
    here = place_ref[0]
    parts = (
        (here ^ 1, mate_ref, (mate_ref, sizes.first_end)),
        (here ^ 3, cross_ref, (cross_late_ref, 0)),
        (here ^ 2, other_ref, (other_late_ref, 0)),
        (here, own_ref, (own_ref, sizes.first_end)),
    )
    copies[0].wait()
    copies[1].wait()
    for head, message, _ in parts:
        for c in range(blocks):
            at = span(head * width + c * LANES, LANES, LANES)
            message[c * tokens : (c + 1) * tokens] = key_ref[:, at]
    rates = rate_ref[...]
    row = lax.broadcasted_iota(jnp.int32, rates.shape, 0)
    copies[2].wait()
    for head, message, _ in parts:
        rate = jnp.sum(jnp.where(row == head, rates, 0.0), axis=0, keepdims=True)
        rate = jnp.broadcast_to(rate, (LANES, tokens)).T
        for c in range(blocks):
            at = span(head * width + c * LANES, LANES, LANES)
            start = sizes.target_at + c * tokens
            value = value_ref[:, at].astype(jnp.float32)
            message[start : start + tokens] = (-(rate * value)).astype(jnp.bfloat16)
    copies[3].wait()
    for head, message, (late, late_at) in parts:
        for m in range(2):
            start = sizes.gate_at + m * rows
            message[start : start + rows] = weight_ref[head, m, :, :LANES].astype(jnp.bfloat16)
            for c in range(1, blocks):
                start = late_at + (m * (blocks - 1) + c - 1) * rows
                late[start : start + rows] = weight_ref[
                    head, m, :, c * LANES : (c + 1) * LANES
                ].astype(jnp.bfloat16)
        for c in range(blocks):
            start = sizes.down_at + c * rows
            message[start : start + rows] = weight_ref[
                head, 2, :, c * LANES : (c + 1) * LANES
            ].astype(jnp.bfloat16)
    copies[4].wait()
    for i, head in enumerate((here ^ 1, here ^ 2)):
        for c in range(blocks):
            at = span(head * width + c * LANES, LANES, LANES)
            start = sizes.query_at + (i * blocks + c) * tokens
            mate_ref[start : start + tokens] = queries_ref[:, at]
    for i, head in enumerate((here, here ^ 3)):
        query_ref[i] = queries_ref[:, span(head * width, width, LANES)]


def pre_grads(pre, back, half):
    gate_pre, up_pre = pre[:, :half], pre[:, half:]
    sig_gate = jax.nn.sigmoid(gate_pre)
    activated = gate_pre * sig_gate
    hidden = (activated * up_pre).astype(jnp.bfloat16)
    gate = (back * up_pre * sig_gate * (1.0 + gate_pre * (1.0 - sig_gate))).astype(jnp.bfloat16)
    return hidden, gate, (back * activated).astype(jnp.bfloat16)


def renewal(old, grad):
    old = old.astype(jnp.float32)
    stepped = old - grad
    old_sq = jnp.sum(old * old, axis=0, keepdims=True)
    new_sq = jnp.sum(stepped * stepped, axis=0, keepdims=True)
    return (stepped * jnp.sqrt((old_sq + epsilon) / (new_sq + epsilon))).astype(jnp.bfloat16)


def quarters(here):
    return (here, here ^ 1, here ^ 3, here ^ 2)


def first_kernel(sizes, place_ref, *refs):
    messages = refs[:4]
    keys, targets, down, hidden_ref, first_ref, weights, gates = refs[4:]
    tokens, rows, blocks = sizes.tokens, sizes.rows, sizes.blocks
    for g, (source, message) in enumerate(zip(quarters(place_ref[0]), messages)):
        at = span(source * rows, rows, 16)
        mine = slice(g * tokens, (g + 1) * tokens)
        for m in range(2):
            start = sizes.gate_at + m * rows
            weights[at, m * LANES : (m + 1) * LANES] = message[start : start + rows]
        for c in range(blocks):
            lanes = slice(c * LANES, (c + 1) * LANES)
            keys[mine, lanes] = message[c * tokens : (c + 1) * tokens]
            start = sizes.target_at + c * tokens
            targets[mine, lanes] = message[start : start + tokens]
            start = sizes.down_at + c * rows
            down[at, lanes] = message[start : start + rows]
    for g in range(4):
        mine = slice(g * tokens, (g + 1) * tokens)
        pre = plain_dot(keys[mine], weights[...])
        back = columns_dot(targets[mine], down[:LANES])
        hidden_ref[mine], gates[mine, :LANES], gates[mine, LANES:] = pre_grads(pre, back, LANES)
    first_ref[...] = renewal(weights[...], rows_dot(keys[...], gates[...]))


def second_kernel(sizes, place_ref, *refs):
    keys, targets, down, early, first, own, mate, cross, other = refs[:9]
    late_ref, down_ref, near_ref, far_ref, far0_ref, far1_ref, same_ref, mate_ref = refs[9:17]
    weights, gates, hidden = refs[17:]
    tokens, rows, blocks, late = sizes.tokens, sizes.rows, sizes.blocks, sizes.late_width
    here = place_ref[0]
    starts = (sizes.first_end, sizes.first_end, 0, 0)
    for source, message, start in zip(quarters(here), (own, mate, cross, other), starts):
        at = span(source * rows, rows, 16)
        for i in range(2 * (blocks - 1)):
            weights[at, i * LANES : (i + 1) * LANES] = message[
                start + i * rows : start + (i + 1) * rows
            ]
    hidden[:, :LANES] = early[...]
    for g in range(4):
        mine = slice(g * tokens, (g + 1) * tokens)
        pre = plain_dot(keys[mine], weights[...])
        back = columns_dot(targets[mine], down[LANES:])
        hidden[mine, LANES:], gates[mine, :late], gates[mine, late:] = pre_grads(pre, back, late)
    late_ref[...] = renewal(weights[...], rows_dot(keys[...], gates[...]))
    down_ref[...] = renewal(down[...], rows_dot(hidden[...], targets[...]))
    half = lax.shift_right_logical(here, 1)
    near = span((1 - half) * 2 * rows, 2 * rows, 16)
    far = span(half * 2 * rows, 2 * rows, 16)
    near_ref[:, : 2 * late] = late_ref[near]
    near_ref[:, 2 * late :] = down_ref[near]
    far_ref[...] = late_ref[far]
    far0_ref[...] = down_ref[far, :late]
    far1_ref[...] = down_ref[far, late:]
    for ref, row in ((same_ref, here), (mate_ref, here ^ 1)):
        at = span(row * rows, rows, 16)
        hand_rows(ref, at, first, late_ref, late)
        ref[2] = down_ref[at]


def hand_rows(ref, at, first, second, late):
    for m in range(2):
        ref[m, :, :LANES] = first[at, m * LANES : (m + 1) * LANES]
        ref[m, :, LANES:] = second[at, m * late : (m + 1) * late]


def hidden_of(query, first, second, late):
    pre, pre_late = plain_dot(query, first[...]), plain_dot(query, second[...])
    gate, up = pre[:, :LANES], pre[:, LANES:]
    gate_late, up_late = pre_late[:, :late], pre_late[:, late:]
    return (
        (gate * jax.nn.sigmoid(gate) * up).astype(jnp.bfloat16),
        (gate_late * jax.nn.sigmoid(gate_late) * up_late).astype(jnp.bfloat16),
    )


def mate_query(sizes, mate, i):
    tokens, blocks = sizes.tokens, sizes.blocks
    start = sizes.query_at + i * blocks * tokens
    return jnp.concatenate(
        [mate[start + c * tokens : start + (c + 1) * tokens] for c in range(blocks)], axis=1
    )


def own_kernel(sizes, place_ref, query, mate, first, second, down, own_ref, mate_ref):
    late = sizes.late_width
    for tokens, ref in ((mate_query(sizes, mate, 0), mate_ref), (query[0], own_ref)):
        early, after = hidden_of(tokens, first, second, late)
        result = plain_dot(early, down[:LANES]) + plain_dot(after, down[LANES:])
        ref[...] = result.astype(jnp.bfloat16)


def rows_kernel(sizes, place_ref, first, near, same_ref, mate_ref):
    late, rows, here = sizes.late_width, sizes.rows, place_ref[0]
    for ref, row in ((mate_ref, here ^ 1), (same_ref, here)):
        at = span(row * rows, rows, 16)
        arrived = span((row & 1) * rows, rows, 16)
        for m in range(2):
            ref[m, :, :LANES] = first[at, m * LANES : (m + 1) * LANES]
            ref[m, :, LANES:] = near[arrived, m * late : (m + 1) * late]
        ref[2] = near[arrived, 2 * late :]


def halves(sizes, here):
    half, rows = lax.shift_right_logical(here, 1), 2 * sizes.rows
    return span(half * rows, rows, 16), span((1 - half) * rows, rows, 16)


def other_kernel(sizes, place_ref, query, mate, first, near, far, hidden_ref, second):
    late, tokens = sizes.late_width, sizes.tokens
    near_at, far_at = halves(sizes, place_ref[0])
    second[near_at] = near[:, : 2 * late]
    second[far_at] = far[...]
    for g, q in enumerate((mate_query(sizes, mate, 1), query[1])):
        mine = slice(g * tokens, (g + 1) * tokens)
        hidden_ref[mine, :LANES], hidden_ref[mine, LANES:] = hidden_of(q, first, second, late)


def result_kernel(sizes, start, place_ref, hidden, near, far, own_ref, mate_ref, down):
    tokens, columns = sizes.tokens, far.shape[-1]
    start += 2 * sizes.late_width
    near_at, far_at = halves(sizes, place_ref[0])
    down[near_at] = near[:, start : start + columns]
    down[far_at] = far[...]
    mate_ref[...] = plain_dot(hidden[:tokens], down[...]).astype(jnp.bfloat16)
    own_ref[...] = plain_dot(hidden[tokens:], down[...]).astype(jnp.bfloat16)


def handed_kernel(place_ref, *refs):
    here = place_ref[0]
    for head, ref in zip((here, here ^ 1, here ^ 3, here ^ 2), refs[:4]):
        refs[4][0, head] = ref[...].astype(jnp.float32)


def applied_kernel(sizes, place_ref, own, mate, own0, own1, mate0, mate1, applied_ref):
    here, width, late = place_ref[0], sizes.width, sizes.late_width
    applied_ref[:, span(here * width, width, LANES)] = own[...]
    applied_ref[:, span((here ^ 1) * width, width, LANES)] = mate[...]
    for head, (first, second) in ((here ^ 3, (own0, own1)), (here ^ 2, (mate0, mate1))):
        applied_ref[:, span(head * width, late, LANES)] = first[...]
        applied_ref[:, span(head * width + late, LANES, LANES)] = second[...]


def head_body(queries, key_rows, value_rows, step_rates, fast_in):
    _, heads, matrices, rows, width = fast_in.shape
    tokens = queries.shape[0]
    blocks = lax.axis_size("block")
    place = lax.axis_index("tok").astype(jnp.int32)[None]
    sizes = Sizes(tokens, rows, width)
    late = sizes.late_width
    flops = 2 * tokens * width * width

    def bf16(*shape):
        return jax.ShapeDtypeStruct(shape, jnp.bfloat16)

    def swapped(value, mask):
        return lax.ppermute(value, "tok", [(i, i ^ mask) for i in range(heads)])

    def next_block(value, mask):
        route = [
            (b * heads + z, ((b + 1) % blocks) * heads + (z ^ mask))
            for b in range(blocks)
            for z in range(heads)
        ]
        return lax.ppermute(value, ("block", "tok"), route)

    arrays = (step_rates.T, key_rows, value_rows, fast_in[0], queries)
    own, mate, cross, cross_late, other, other_late, query = call(
        functools.partial(pack_kernel, sizes),
        [
            bf16(sizes.query_at, LANES),
            bf16(sizes.mate_end, LANES),
            bf16(sizes.first_end, LANES),
            bf16(sizes.late, LANES),
            bf16(sizes.first_end, LANES),
            bf16(sizes.late, LANES),
            bf16(2, tokens, width),
        ],
        [pltpu.VMEM(a.shape, a.dtype) for a in arrays] + [pltpu.SemaphoreType.DMA((5,))],
        place,
        arrays,
        kept=range(5),
        limit=40,
    )
    mate = swapped(mate, 1)
    cross = swapped(cross, 3)
    other = swapped(other, 2)
    cross_late = swapped(cross_late, 3)
    other_late = swapped(other_late, 2)

    keys, targets, down, early, first = call(
        functools.partial(first_kernel, sizes),
        [
            bf16(heads * tokens, width),
            bf16(heads * tokens, width),
            bf16(width, width),
            bf16(heads * tokens, LANES),
            bf16(width, 2 * LANES),
        ],
        [
            pltpu.VMEM((width, 2 * LANES), jnp.bfloat16),
            pltpu.VMEM((heads * tokens, 2 * LANES), jnp.bfloat16),
        ],
        place,
        (own, mate, cross, other),
        6 * heads * flops // 3,
    )
    first_in = swapped(first, 3)
    second, down, near, far, far0, far1, same_rows, mate_rows = call(
        functools.partial(second_kernel, sizes),
        [
            bf16(width, 2 * late),
            bf16(width, width),
            bf16(2 * rows, 2 * late + width),
            bf16(2 * rows, 2 * late),
            bf16(2 * rows, late),
            bf16(2 * rows, LANES),
            bf16(matrices, rows, width),
            bf16(matrices, rows, width),
        ],
        [
            pltpu.VMEM((width, 2 * late), jnp.bfloat16),
            pltpu.VMEM((heads * tokens, 2 * late), jnp.bfloat16),
            pltpu.VMEM((heads * tokens, width), jnp.bfloat16),
        ],
        place,
        (keys, targets, down, early, first, own, mate, cross_late, other_late),
        12 * heads * flops // 3,
    )
    near_in = swapped(near, 3)
    far_in = swapped(far, 3)
    far0_in = swapped(far0, 3)
    far1_in = swapped(far1, 3)
    own_result, mate_result = call(
        functools.partial(own_kernel, sizes),
        [bf16(tokens, width)] * 2,
        [],
        place,
        (query, mate, first, second, down),
        6 * flops,
    )
    mate_result = swapped(mate_result, 1)
    handed_own = next_block(same_rows, 0)
    handed_mate = next_block(mate_rows, 1)

    same_rows, mate_rows = call(
        functools.partial(rows_kernel, sizes),
        [bf16(matrices, rows, width)] * 2,
        [],
        place,
        (first_in, near_in),
    )
    handed_cross = next_block(mate_rows, 1)
    handed_other = next_block(same_rows, 0)
    (hidden,) = call(
        functools.partial(other_kernel, sizes),
        [bf16(2 * tokens, width)],
        [pltpu.VMEM((width, 2 * late), jnp.bfloat16)],
        place,
        (query, mate, first_in, near_in, far_in),
        4 * flops,
    )
    own_parts, mate_parts = [], []
    for i, far in enumerate((far0_in, far1_in)):
        columns = far.shape[-1]
        own_part, mate_part = call(
            functools.partial(result_kernel, sizes, i * late),
            [bf16(tokens, columns)] * 2,
            [pltpu.VMEM((width, columns), jnp.bfloat16)],
            place,
            (hidden, near_in, far),
            2 * flops * columns // width,
        )
        own_parts.append(own_part)
        mate_parts.append(swapped(mate_part, 1))
    (handed,) = call(
        handed_kernel,
        [jax.ShapeDtypeStruct((1, heads, matrices, rows, width), jnp.float32)],
        [],
        place,
        (handed_own, handed_mate, handed_other, handed_cross),
    )
    (applied,) = call(
        functools.partial(applied_kernel, sizes),
        [bf16(tokens, heads * width)],
        [],
        place,
        (own_result, mate_result, *own_parts, *mate_parts),
    )
    return (applied, handed)


def body(queries, key_rows, value_rows, step_rates, fast_in):
    by_head = fast_in.shape[1] == lax.axis_size("tok") == 4
    chosen = head_body if by_head else gathered_body
    return chosen(queries, key_rows, value_rows, step_rates, fast_in)


def solution(mesh):
    return jax.shard_map(
        body,
        mesh=mesh,
        in_specs=(
            P(("block", "tok"), None),
            P(("block", "tok"), None),
            P(("block", "tok"), None),
            P(("block", "tok"), None),
            P("block", None, None, "tok", None),
        ),
        out_specs=(P(("block", "tok"), None), P("block", None, None, "tok", None)),
        check_vma=False,
    )
```
